32 devices in a mesh: seq: 8 (over y, x, core), wshard: 4 (over z).
Axes of the slice: x: 2, y: 2, z: 4, core: 2. Of those that a mesh axis runs over, the one named last changes fastest.
Arguments:
- tokens: float32 [6144, 768], P(('seq', 'wshard')), may hold values from -18 to 18, as said below
- attention_norm_gain: float32 [2, 768], replicated, may hold values from 0.5 to 1.5
- qkv_weight: bfloat16 [2, 768, 2304], P(None, None, 'wshard'), may hold values from -7 to 7, as said below
- output_weight: bfloat16 [2, 768, 768], P(None, None, 'wshard'), may hold values from -0.75 to 0.75
- feedforward_norm_gain: float32 [2, 768], replicated, may hold values from 0.5 to 1.5
- input_weight: bfloat16 [2, 768, 2304], P(None, None, 'wshard'), may hold values from -0.21875 to 0.21875
- down_weight: bfloat16 [2, 1152, 768], P(None, 'wshard'), may hold values from -0.1875 to 0.1875
- cotangent: float32 [6144, 768], P(('seq', 'wshard')), may hold values from -18 to 18
Outputs:
- outputs: float32 [6144, 768], P(('seq', 'wshard'))
- input_grad: float32 [6144, 768], P(('seq', 'wshard'))
- grad_attention_gain: float32 [2, 768], replicated
- grad_qkv_weight: float32 [2, 768, 2304], P(None, 'seq', 'wshard')
- grad_output_weight: float32 [2, 768, 768], P(None, 'seq', 'wshard')
- grad_feedforward_gain: float32 [2, 768], replicated
- grad_input_weight: float32 [2, 768, 2304], P(None, 'seq', 'wshard')
- grad_down_weight: float32 [2, 1152, 768], P(None, 'wshard', 'seq')
The draws below stay inside these ranges and needn't reach their ends.
Inputs may be any that keep to these rules, and one draw needn't show every extreme that they name: `tokens`: activations of the first layer. `qkv_weight`: columns hold queries, keys, values, each head by head.
All inputs are finite; a program needn't handle non-finite values.
Results may differ from the reference program's by a relative error of at most 0.022.
Values may be sent and summed in bfloat16 or wider, within the bound.
A program may use at most 192 MiB of HBM per device.

```python
import math
from functools import partial
import jax
import jax.numpy as jnp
from jax import lax

D = 768
HEADS = 12
HDIM = 64
FF = 1152
WIN = 64
LAYERS = 2
SEQS = 1
TOK_DEV = 192
TOKENS = 6144


def draw_tokens(key, part):
    columns = jnp.exp(jax.random.uniform(jax.random.fold_in(key, 12), (1, D), jnp.float32, math.log(0.3), math.log(3.0)))
    noise = jnp.clip(jax.random.normal(jax.random.fold_in(key, 11), (TOKENS, D), jnp.float32), -6.0, 6.0)
    return (noise * columns).astype(jnp.float32)


def draw_cotangent(key, part):
    along = jnp.arange(TOKENS, dtype=jnp.float32) * (1.0 / TOKENS)
    noise = jnp.clip(jax.random.normal(jax.random.fold_in(key, 21), (TOKENS, D), jnp.float32), -6.0, 6.0)
    rising = jnp.exp(math.log(3.0) * along)[:, None]
    return (noise * rising).astype(jnp.float32)


def draw_qkv_weight(key, part):
    base = jnp.clip(jax.random.normal(jax.random.fold_in(key, 31), (LAYERS, D, 3 * D), jnp.float32), -6.0, 6.0) * D ** (-0.5)
    return base.astype(jnp.bfloat16)


def shard_levels(own_key, shape, shards, low, top_value):
    def one(axis_at, parts):
        heights = jax.random.uniform(jax.random.fold_in(jax.random.fold_in(own_key, 6), axis_at), (parts,), jnp.float32, low / len(shards), top_value / len(shards))
        return jnp.repeat(jnp.exp(heights), shape[axis_at] // parts).reshape((-1,) + (1,) * (len(shape) - axis_at - 1))

    loudness = one(*shards[0])
    for cut in shards[1:]:
        loudness = loudness * one(*cut)
    return loudness


def normal_values(rng, dims, spread, reach, shards=(), kind=jnp.bfloat16):
    gain = shard_levels(rng, dims, shards, -0.22, 0.18) if shards else 1.0
    values = jax.random.normal(rng, dims, jnp.float32) * spread * gain
    return jnp.minimum(jnp.maximum(values, -reach), reach).astype(kind)


def setup_inputs(seed: int = 0) -> dict:
    seeds = jax.random.split(jax.random.key(seed), 9)
    tokens = draw_tokens(jax.random.fold_in(seeds[8], 71), 0)
    attention_norm_gain = jnp.clip(1.0 + 0.1 * jax.random.normal(seeds[1], (LAYERS, D), jnp.float32), 0.5, 1.5)
    qkv_weight = draw_qkv_weight(jax.random.fold_in(seeds[8], 71), 0)
    output_weight = normal_values(seeds[3], (LAYERS, D, D), HDIM ** -0.5, 0.75, ((2, 4),))
    feedforward_norm_gain = jnp.clip(1.0 + 0.1 * jax.random.normal(seeds[4], (LAYERS, D), jnp.float32), 0.5, 1.5)
    input_weight = normal_values(seeds[5], (LAYERS, D, 2 * FF), D ** -0.5, 0.21875, ((2, 4),))
    down_weight = normal_values(seeds[6], (LAYERS, FF, D), FF ** -0.5, 0.1875, ((1, 4),))
    cotangent = draw_cotangent(jax.random.fold_in(seeds[8], 71), 0)
    return dict(tokens=tokens, attention_norm_gain=attention_norm_gain, qkv_weight=qkv_weight, output_weight=output_weight, feedforward_norm_gain=feedforward_norm_gain, input_weight=input_weight, down_weight=down_weight, cotangent=cotangent)


EPSILON = 1e-05
THETA = 10000.0

def rotate_half(values):
    middle_state = values.shape[-1] // 2
    return jnp.concatenate([-values[..., middle_state:], values[..., :middle_state]], axis=-1)

def rope_tables(positions):
    middle_state = HDIM // 2
    inverse = THETA ** (-(jnp.arange(middle_state, dtype=jnp.float32) * (2.0 / HDIM)))
    angles = positions.astype(jnp.float32)[:, None] * inverse[None, :]
    cosine = jnp.concatenate([jnp.cos(angles), jnp.cos(angles)], axis=1)
    sine = jnp.concatenate([jnp.sin(angles), jnp.sin(angles)], axis=1)
    return (cosine[:, None, :], sine[:, None, :])

def apply_rope(values, cosine, sine):
    return values * cosine + rotate_half(values) * sine

def undo_rope(grads, cosine, sine):
    return grads * cosine - rotate_half(grads * sine)

def layer_normalize(hidden_state):
    centred = hidden_state - lax.optimization_barrier(jnp.mean(hidden_state, axis=-1, keepdims=True))
    inverse = lax.rsqrt(lax.optimization_barrier(jnp.mean(centred * centred, axis=-1, keepdims=True)) + EPSILON)
    return (centred * inverse, inverse)

def norm_backward_step(normalized_gradient, normed, inverse, gain_row):
    scaled = normalized_gradient * gain_row
    result = scaled - lax.optimization_barrier(jnp.mean(scaled, axis=-1, keepdims=True)) - normed * lax.optimization_barrier(jnp.mean(scaled * normed, axis=-1, keepdims=True))
    return (result * inverse, lax.optimization_barrier(jnp.sum(normalized_gradient * normed, axis=0)))

def gelu_exact(inner_activation):
    return 0.5 * inner_activation * (1.0 + lax.erf(inner_activation * (1.0 / math.sqrt(2.0))))

def gelu_slope(inner_activation):
    return 0.5 * (1.0 + lax.erf(inner_activation * (1.0 / math.sqrt(2.0)))) + inner_activation * jnp.exp(-0.5 * inner_activation * inner_activation) * (1.0 / math.sqrt(2.0 * math.pi))

def band_mask(query_pos, key_pos, length):
    near = jnp.abs(query_pos[:, None] - key_pos[None, :]) <= WIN
    same = query_pos[:, None] // length == key_pos[None, :] // length
    return near & same

def block_scores(query_matrix, key_rows, allowed):
    scores = jnp.einsum('qhd,khd->hqk', query_matrix.astype(jnp.float32), key_rows.astype(jnp.float32)) * (1.0 / math.sqrt(HDIM))
    return jnp.where(allowed[None], scores, -1e+30)

def forward_block(query_matrix, padded_keys, padded_values, block, length, index):
    start = index * block
    query_rows = lax.dynamic_slice_in_dim(query_matrix, start, block, 0)
    key_rows = lax.dynamic_slice_in_dim(padded_keys, start, block + 2 * WIN, 0)
    value_rows = lax.dynamic_slice_in_dim(padded_values, start, block + 2 * WIN, 0)
    query_pos = start + jnp.arange(block, dtype=jnp.int32)
    key_pos = start - WIN + jnp.arange(block + 2 * WIN, dtype=jnp.int32)
    scores = block_scores(query_rows, key_rows, band_mask(query_pos, key_pos, length))
    top = lax.optimization_barrier(jnp.max(scores, axis=-1, keepdims=True))
    log_total = top + jnp.log(lax.optimization_barrier(jnp.sum(jnp.exp(scores - top), axis=-1, keepdims=True)))
    probs = jnp.exp(scores - log_total).astype(jnp.bfloat16)
    context_rows = jnp.einsum('hqk,khd->qhd', probs.astype(jnp.float32), value_rows.astype(jnp.float32)).astype(jnp.bfloat16)
    return (context_rows, log_total)

def back_block(query_matrix, padded_keys, padded_values, logsumexp_totals, grad_context, block, length, carry, index):
    grad_key_pad, grad_value_pad = carry
    start = index * block
    query_rows = lax.dynamic_slice_in_dim(query_matrix, start, block, 0)
    key_rows = lax.dynamic_slice_in_dim(padded_keys, start, block + 2 * WIN, 0)
    value_rows = lax.dynamic_slice_in_dim(padded_values, start, block + 2 * WIN, 0)
    grad_rows = lax.dynamic_slice_in_dim(grad_context, start, block, 0).astype(jnp.float32)
    query_pos = start + jnp.arange(block, dtype=jnp.int32)
    key_pos = start - WIN + jnp.arange(block + 2 * WIN, dtype=jnp.int32)
    scores = block_scores(query_rows, key_rows, band_mask(query_pos, key_pos, length))
    probs = jnp.exp(scores - logsumexp_totals[index])
    grad_values = jnp.einsum('hqk,qhd->khd', probs.astype(jnp.bfloat16).astype(jnp.float32), grad_rows)
    grad_probs = jnp.einsum('qhd,khd->hqk', grad_rows, value_rows.astype(jnp.float32))
    grad_scores = (probs * (grad_probs - lax.optimization_barrier(jnp.sum(probs * grad_probs, axis=-1, keepdims=True))) * (1.0 / math.sqrt(HDIM))).astype(jnp.bfloat16).astype(jnp.float32)
    grad_queries = jnp.einsum('hqk,khd->qhd', grad_scores, key_rows.astype(jnp.float32))
    grad_keys = jnp.einsum('hqk,qhd->khd', grad_scores, query_rows.astype(jnp.float32))
    old_keys = lax.dynamic_slice_in_dim(grad_key_pad, start, block + 2 * WIN, 0)
    old_values = lax.dynamic_slice_in_dim(grad_value_pad, start, block + 2 * WIN, 0)
    grad_key_pad = lax.dynamic_update_slice_in_dim(grad_key_pad, old_keys + grad_keys, start, 0)
    grad_value_pad = lax.dynamic_update_slice_in_dim(grad_value_pad, old_values + grad_values, start, 0)
    return ((grad_key_pad, grad_value_pad), grad_queries)

def reference(tokens, attention_norm_gain, qkv_weight, output_weight, feedforward_norm_gain, input_weight, down_weight, cotangent):
    length = TOKENS // SEQS
    positions = jnp.arange(TOKENS, dtype=jnp.int32)
    cosine, sine = rope_tables(positions % length)
    block = 512 if TOKENS % 512 == 0 else TOK_DEV
    count = TOKENS // block
    indices = jnp.arange(count, dtype=jnp.int32)
    scale_grad = 1.0 / math.sqrt(TOKENS)
    hidden_state = tokens
    saved_activations = []
    for layer_number in range(LAYERS):
        attention_standardized, attention_inverse_deviation = layer_normalize(hidden_state)
        attention_normalized = (attention_standardized * attention_norm_gain[layer_number]).astype(jnp.bfloat16)
        qkv = jnp.dot(attention_normalized, qkv_weight[layer_number], preferred_element_type=jnp.float32)
        query_matrix = apply_rope(qkv[:, :D].reshape(TOKENS, HEADS, HDIM), cosine, sine).astype(jnp.bfloat16)
        key_rows = apply_rope(qkv[:, D:2 * D].reshape(TOKENS, HEADS, HDIM), cosine, sine).astype(jnp.bfloat16)
        value_rows = qkv[:, 2 * D:].reshape(TOKENS, HEADS, HDIM).astype(jnp.bfloat16)
        padded_keys = jnp.pad(key_rows, ((WIN, WIN), (0, 0), (0, 0)))
        padded_values = jnp.pad(value_rows, ((WIN, WIN), (0, 0), (0, 0)))
        contexts, logsumexp_totals = lax.map(partial(forward_block, query_matrix, padded_keys, padded_values, block, length), indices)
        context_rows = contexts.reshape(TOKENS, D)
        middle_state = hidden_state + jnp.dot(context_rows, output_weight[layer_number], preferred_element_type=jnp.float32)
        feedforward_standardized, feedforward_inverse_deviation = layer_normalize(middle_state)
        feedforward_normalized = (feedforward_standardized * feedforward_norm_gain[layer_number]).astype(jnp.bfloat16)
        inner_activation = jnp.dot(feedforward_normalized, input_weight[layer_number], preferred_element_type=jnp.float32)
        gated_linear_output = (gelu_exact(inner_activation[:, :FF]) * inner_activation[:, FF:]).astype(jnp.bfloat16)
        saved_activations.append((attention_standardized, attention_inverse_deviation, attention_normalized, query_matrix, padded_keys, padded_values, logsumexp_totals, context_rows, feedforward_standardized, feedforward_inverse_deviation, feedforward_normalized, inner_activation, gated_linear_output))
        hidden_state = middle_state + jnp.dot(gated_linear_output, down_weight[layer_number], preferred_element_type=jnp.float32)
    outputs = hidden_state
    grad = cotangent
    list_again, list_qkv, list_out, list_fgain, list_in, list_down = ([], [], [], [], [], [])
    for layer_number in reversed(range(LAYERS)):
        attention_standardized, attention_inverse_deviation, attention_normalized, query_matrix, padded_keys, padded_values, logsumexp_totals, context_rows, feedforward_standardized, feedforward_inverse_deviation, feedforward_normalized, inner_activation, gated_linear_output = saved_activations[layer_number]
        grad_rounded = grad.astype(jnp.bfloat16)
        list_down.append(jnp.dot(gated_linear_output.T, grad_rounded, preferred_element_type=jnp.float32) * scale_grad)
        grad_geglu = jnp.dot(grad_rounded, down_weight[layer_number].T, preferred_element_type=jnp.float32)
        gate = inner_activation[:, :FF]
        upper = inner_activation[:, FF:]
        grad_inner = jnp.concatenate([grad_geglu * upper * gelu_slope(gate), grad_geglu * gelu_exact(gate)], axis=1).astype(jnp.bfloat16)
        list_in.append(jnp.dot(feedforward_normalized.T, grad_inner, preferred_element_type=jnp.float32) * scale_grad)
        normalized_gradient = jnp.dot(grad_inner, input_weight[layer_number].T, preferred_element_type=jnp.float32)
        partial_gradient, feedforward_gain_gradient = norm_backward_step(normalized_gradient, feedforward_standardized, feedforward_inverse_deviation, feedforward_norm_gain[layer_number])
        list_fgain.append(feedforward_gain_gradient * scale_grad)
        grad_middle = grad + partial_gradient
        grad_middle_rounded = grad_middle.astype(jnp.bfloat16)
        list_out.append(jnp.dot(context_rows.T, grad_middle_rounded, preferred_element_type=jnp.float32) * scale_grad)
        grad_context = jnp.dot(grad_middle_rounded, output_weight[layer_number].T, preferred_element_type=jnp.float32).astype(jnp.bfloat16).reshape(TOKENS, HEADS, HDIM)
        empty = jnp.zeros((TOKENS + 2 * WIN, HEADS, HDIM), jnp.float32)
        (grad_key_pad, grad_value_pad), grad_queries = lax.scan(partial(back_block, query_matrix, padded_keys, padded_values, logsumexp_totals, grad_context, block, length), (empty, empty), indices)
        grad_queries = grad_queries.reshape(TOKENS, HEADS, HDIM)
        grad_keys = grad_key_pad[WIN:WIN + TOKENS]
        grad_values = grad_value_pad[WIN:WIN + TOKENS]
        grad_qkv = jnp.concatenate([undo_rope(grad_queries, cosine, sine).reshape(TOKENS, D), undo_rope(grad_keys, cosine, sine).reshape(TOKENS, D), grad_values.reshape(TOKENS, D)], axis=1).astype(jnp.bfloat16)
        list_qkv.append(jnp.dot(attention_normalized.T, grad_qkv, preferred_element_type=jnp.float32) * scale_grad)
        attention_normalized_gradient = jnp.dot(grad_qkv, qkv_weight[layer_number].T, preferred_element_type=jnp.float32)
        attention_partial_gradient, attention_gain_gradient = norm_backward_step(attention_normalized_gradient, attention_standardized, attention_inverse_deviation, attention_norm_gain[layer_number])
        list_again.append(attention_gain_gradient * scale_grad)
        grad = grad_middle + attention_partial_gradient
    return (outputs, grad, jnp.stack(list_again[::-1]), jnp.stack(list_qkv[::-1]), jnp.stack(list_out[::-1]), jnp.stack(list_fgain[::-1]), jnp.stack(list_in[::-1]), jnp.stack(list_down[::-1]))
```

```python
import math

import jax
import jax.numpy as jnp
from jax import lax
from jax.experimental import pallas as pl
from jax.experimental.pallas import tpu as pltpu
from jax.sharding import PartitionSpec as P

D = 768
HEADS = 12
HDIM = 64
FF = 1152
WIN = 64
LAYERS = 2
SEQS = 1


EPSILON = 1e-05
THETA = 10000.0


def with_halo(cells, sides, width):
    for axis, dim in sides:
        count = lax.axis_size(axis)
        ends = count - 1
        head = lax.slice_in_dim(cells, 0, width, axis=dim)
        tail = lax.slice_in_dim(cells, cells.shape[dim] - width, cells.shape[dim], axis=dim)
        cells = jnp.concatenate(
            [
                lax.ppermute(tail, axis, [(i, (i + 1) % count) for i in range(ends)]),
                cells,
                lax.ppermute(head, axis, [((i + 1) % count, i) for i in range(ends)]),
            ],
            axis=dim,
        )
    return cells


def rope_tables(positions):
    middle_state = HDIM // 2
    inverse = THETA ** (-(jnp.arange(middle_state, dtype=jnp.float32) * (2.0 / HDIM)))
    angles = positions.astype(jnp.float32)[:, None] * inverse[None, :]
    return (
        jnp.concatenate([jnp.cos(angles)] * 4, axis=1),
        jnp.concatenate([jnp.sin(angles)] * 4, axis=1),
    )


def layer_normalize(hidden_state):
    centred = hidden_state - jnp.mean(hidden_state, axis=-1, keepdims=True)
    inverse = lax.rsqrt(jnp.mean(centred * centred, axis=-1, keepdims=True) + EPSILON)
    return (centred * inverse, inverse)


def norm_backward_step(normalized_gradient, normed, inverse, gain_row):
    scaled = normalized_gradient * gain_row
    result = (
        scaled
        - jnp.mean(scaled, axis=-1, keepdims=True)
        - normed * jnp.mean(scaled * normed, axis=-1, keepdims=True)
    )
    return (result * inverse, jnp.sum(normalized_gradient * normed, axis=0))


def gelu_exact(inner_activation):
    return 0.5 * inner_activation * (1.0 + lax.erf(inner_activation * (1.0 / math.sqrt(2.0))))


def gelu_slope(inner_activation):
    return 0.5 * (
        1.0 + lax.erf(inner_activation * (1.0 / math.sqrt(2.0)))
    ) + inner_activation * jnp.exp(-0.5 * inner_activation * inner_activation) * (
        1.0 / math.sqrt(2.0 * math.pi)
    )


def lane_half(shape):
    return lax.rem(lax.broadcasted_iota(jnp.int32, shape, 1), HDIM) < HDIM // 2


def rotate_lanes(values, sign):
    width = values.shape[1]
    ahead = pltpu.roll(values, width - HDIM // 2, 1)
    behind = pltpu.roll(values, HDIM // 2, 1)
    return jnp.where(lane_half(values.shape), -sign * ahead, sign * behind)


def spread(table):
    return jnp.concatenate([table] * (D // table.shape[1]), axis=1)


def rope_kernel(qkv_ref, cosine_ref, sine_ref, query_ref, kv_ref):
    cosine = spread(cosine_ref[...])
    sine = spread(sine_ref[...])
    queries = qkv_ref[:, :D]
    keys = qkv_ref[:, D : 2 * D]
    query_ref[...] = (queries * cosine + rotate_lanes(queries, 1.0) * sine).astype(jnp.bfloat16)
    kv_ref[:, :D] = (keys * cosine + rotate_lanes(keys, 1.0) * sine).astype(jnp.bfloat16)
    kv_ref[:, D:] = qkv_ref[:, 2 * D :].astype(jnp.bfloat16)


def dot_f32(left, right, dims):
    return lax.dot_general(left, right, (dims, ((), ())), preferred_element_type=jnp.float32)


def head_scores(queries, keys, allowed):
    scores = dot_f32(queries, keys, ((1,), (1,))) * (1.0 / math.sqrt(HDIM))
    return jnp.where(allowed, scores, -1e30)


def window_mask(bounds_ref, rows):
    shape = (rows, rows + 2 * WIN)
    query = lax.broadcasted_iota(jnp.int32, shape, 0)
    key = lax.broadcasted_iota(jnp.int32, shape, 1)
    near = (key >= query) & (key <= query + 2 * WIN)
    return near & (key >= bounds_ref[0]) & (key < bounds_ref[1])


def forward_kernel(bounds_ref, query_ref, kv_ref, context_ref, log_ref):
    rows = query_ref.shape[0]
    allowed = window_mask(bounds_ref, rows)
    logs = []
    for head in range(HEADS):
        cols = slice(head * HDIM, (head + 1) * HDIM)
        shifted = slice(D + head * HDIM, D + (head + 1) * HDIM)
        scores = head_scores(query_ref[:, cols], kv_ref[:, cols], allowed)
        top = jnp.max(scores, axis=1, keepdims=True)
        log_total = top + jnp.log(jnp.sum(jnp.exp(scores - top), axis=1, keepdims=True))
        probs = jnp.exp(scores - log_total).astype(jnp.bfloat16)
        context_ref[:, cols] = dot_f32(probs, kv_ref[:, shifted], ((1,), (0,))).astype(
            jnp.bfloat16
        )
        logs.append(log_total)
    log_ref[...] = jnp.concatenate(logs, axis=1)


def backward_kernel(
    bounds_ref, query_ref, kv_ref, log_ref, grad_ref, dquery_ref, local_ref, rim_ref
):
    rows = query_ref.shape[0]
    allowed = window_mask(bounds_ref, rows)
    for head in range(HEADS):
        cols = slice(head * HDIM, (head + 1) * HDIM)
        shifted = slice(D + head * HDIM, D + (head + 1) * HDIM)
        queries = query_ref[:, cols]
        keys = kv_ref[:, cols]
        grads = grad_ref[:, cols]
        scores = head_scores(queries, keys, allowed)
        probs = jnp.exp(scores - log_ref[:, head : head + 1])
        grad_values = dot_f32(probs.astype(jnp.bfloat16), grads, ((0,), (0,)))
        grad_probs = dot_f32(grads, kv_ref[:, shifted], ((1,), (1,)))
        inner = jnp.sum(probs * grad_probs, axis=1, keepdims=True)
        grad_scores = (probs * (grad_probs - inner) * (1.0 / math.sqrt(HDIM))).astype(jnp.bfloat16)
        dquery_ref[:, cols] = dot_f32(grad_scores, keys, ((1,), (0,)))
        grad_keys = dot_f32(grad_scores, queries, ((0,), (0,)))
        for place, value in ((cols, grad_keys), (shifted, grad_values)):
            local_ref[:, place] = value[WIN : WIN + rows]
            rim_ref[:WIN, place] = value[:WIN].astype(jnp.bfloat16)
            rim_ref[WIN:, place] = value[WIN + rows :].astype(jnp.bfloat16)


def unrope_kernel(dquery_ref, local_ref, low_ref, high_ref, cosine_ref, sine_ref, out_ref):
    rows = dquery_ref.shape[0]
    cosine = spread(cosine_ref[...])
    sine = spread(sine_ref[...])
    queries = dquery_ref[...]
    out_ref[:, :D] = (queries * cosine - rotate_lanes(queries * sine, 1.0)).astype(jnp.bfloat16)
    local = local_ref[...]
    top = jnp.concatenate([low_ref[...].astype(jnp.float32), jnp.zeros((rows - WIN, 2 * D), jnp.float32)], axis=0)
    bottom = jnp.concatenate([jnp.zeros((rows - WIN, 2 * D), jnp.float32), high_ref[...].astype(jnp.float32)], axis=0)
    local = local + top + bottom
    keys = local[:, :D]
    out_ref[:, D : 2 * D] = (keys * cosine - rotate_lanes(keys * sine, 1.0)).astype(jnp.bfloat16)
    out_ref[:, 2 * D :] = local[:, D:].astype(jnp.bfloat16)


def local_call(kernel, outs, flops, operands, scalars=False):
    moved = sum(x.size * x.dtype.itemsize for x in operands) + sum(
        math.prod(shape) * jnp.dtype(kind).itemsize for shape, kind in outs
    )
    specs = [pl.BlockSpec(memory_space=pltpu.VMEM)] * len(operands)
    if scalars:
        specs[0] = pl.BlockSpec(memory_space=pltpu.SMEM)
    return pl.pallas_call(
        kernel,
        out_shape=[jax.ShapeDtypeStruct(shape, kind) for shape, kind in outs],
        in_specs=specs,
        out_specs=[pl.BlockSpec(memory_space=pltpu.VMEM)] * len(outs),
        cost_estimate=pl.CostEstimate(flops=flops, bytes_accessed=moved, transcendentals=0),
        compiler_params=pltpu.CompilerParams(vmem_limit_bytes=40 * 1024 * 1024),
    )(*operands)


MESH = pl.DeviceIdType.MESH


def bit_orders(n_seq):
    bits = n_seq.bit_length() - 1
    upper = list(range(1, bits))
    return upper, upper[::-1]


def bit_of(value, bit):
    return lax.rem(value // (1 << bit), 2)


def flipped(value, bit):
    return value + (1 - 2 * bit_of(value, bit)) * (1 << bit)


def greet(n_seq, n_w, me, w):
    barrier = pltpu.get_barrier_semaphore()
    bits = n_seq.bit_length() - 1
    for bit in range(bits):
        pl.semaphore_signal(
            barrier, inc=1, device_id={"seq": flipped(me, bit)}, device_id_type=MESH
        )
    for j in range(1, n_w):
        pl.semaphore_signal(
            barrier, inc=1, device_id={"wshard": lax.rem(w + j, n_w)}, device_id_type=MESH
        )
    pl.semaphore_wait(barrier, bits + n_w - 1)


def gather_kernel(n_seq, n_w, orders, *refs):
    n = len(orders)
    shares, wholes, stage = refs[:n], refs[n : 2 * n], refs[2 * n : 3 * n]
    load_sem, keep_sem, zsend, zrecv, hsend, hrecv = refs[3 * n :]
    me = lax.axis_index("seq")
    w = lax.axis_index("wshard")
    bits = n_seq.bit_length() - 1
    places = [sum(bit_of(me, bit) * (1 << k) for k, bit in enumerate(order)) for order in orders]
    loads = [pltpu.make_async_copy(shares[c], stage[c], load_sem.at[c]) for c in range(n)]
    keeps = [pltpu.make_async_copy(stage[c], wholes[c].at[w], keep_sem.at[c]) for c in range(n)]
    for copy in loads:
        copy.start()
    greet(n_seq, n_w, me, w)

    def across(c, j):
        place = places[c]
        return pltpu.make_async_remote_copy(
            src_ref=shares[c].at[place],
            dst_ref=wholes[c].at[w, place],
            send_sem=zsend.at[c, j - 1],
            recv_sem=zrecv.at[c, j - 1],
            device_id={"wshard": lax.rem(w + j, n_w)},
            device_id_type=MESH,
        )

    def within(c, k, j):
        base = places[c] // (1 << k) * (1 << k)
        block = wholes[c].at[lax.rem(w - j + n_w, n_w), pl.ds(base, 1 << k)]
        return pltpu.make_async_remote_copy(
            src_ref=block,
            dst_ref=block,
            send_sem=hsend.at[c, k, j - 1],
            recv_sem=hrecv.at[c, k, j - 1],
            device_id={"seq": flipped(me, orders[c][k])},
            device_id_type=MESH,
        )

    def arrived(c, k, j):
        source = lax.rem(w - j + n_w, n_w)
        if k == 0:
            dst = wholes[c].at[source, places[c]]
            sem = zrecv.at[c, j - 1]
        else:
            base = flipped(places[c], k - 1) // (1 << (k - 1)) * (1 << (k - 1))
            dst = wholes[c].at[source, pl.ds(base, 1 << (k - 1))]
            sem = hrecv.at[c, k - 1, j - 1]
        pltpu.make_async_copy(dst, dst, sem).wait()

    for c in range(n):
        for j in range(1, n_w):
            across(c, j).start()
    for c in range(n):
        loads[c].wait()
        keeps[c].start()
    for slot in range(n + bits):
        for k in reversed(range(bits + 1)):
            c = slot - k
            if not 0 <= c < n:
                continue
            for j in range(1, n_w):
                arrived(c, k, j)
                if k < bits:
                    within(c, k, j).start()
    for c in range(n):
        keeps[c].wait()
        for j in range(1, n_w):
            across(c, j).wait_send()
            for k in range(bits):
                within(c, k, j).wait_send()


def gather_weights(shares, orders, n_seq, n_w):
    n = len(shares)
    bits = n_seq.bit_length() - 1
    dma = pltpu.SemaphoreType.DMA
    return pl.pallas_call(
        lambda *refs: gather_kernel(n_seq, n_w, orders, *refs),
        out_shape=[jax.ShapeDtypeStruct((n_w,) + s.shape, s.dtype) for s in shares],
        in_specs=[pl.BlockSpec(memory_space=pl.ANY)] * n,
        out_specs=[pl.BlockSpec(memory_space=pl.ANY)] * n,
        scratch_shapes=[pltpu.VMEM(s.shape, s.dtype) for s in shares]
        + [
            dma((n,)),
            dma((n,)),
            dma((n, n_w - 1)),
            dma((n, n_w - 1)),
            dma((n, bits, n_w - 1)),
            dma((n, bits, n_w - 1)),
        ],
        compiler_params=pltpu.CompilerParams(
            collective_id=0, has_side_effects=True, vmem_limit_bytes=60 * 1024 * 1024
        ),
    )(*shares)


def column_step(width):
    for step in (384, 256, 128):
        if width % step == 0:
            return step
    return width


def sum_kernel(n_seq, n_w, orders, scale, *refs):
    n = len(orders)
    lefts, rights, outs = refs[:n], refs[n : 2 * n], refs[2 * n : 3 * n]
    rest = refs[3 * n :]
    bits = n_seq.bit_length() - 1
    m = bits - 1
    count = 1 << m
    per = 5 + 2 * m
    pools = [rest[c * per : (c + 1) * per] for c in range(n)]
    load_sem, xsend, xrecv, hsend, hrecv, zsend, zrecv = rest[n * per :]
    me = lax.axis_index("seq")
    w = lax.axis_index("wshard")
    peer = flipped(me, 0)

    def strip_of(base, order, i):
        code = count - 1 - i
        for k, bit in enumerate(order):
            if code >> (m - 1 - k) & 1:
                base = flipped(base, bit)
        return base

    def own_loads(c):
        lbuf, rbuf = pools[c][:2]
        for i in range(count):
            yield pltpu.make_async_copy(
                lefts[c].at[strip_of(me, orders[c], i)], lbuf.at[0, i], load_sem.at[c, 0]
            )
        yield pltpu.make_async_copy(rights[c], rbuf.at[0], load_sem.at[c, 1])

    def trades(c):
        lbuf, rbuf = pools[c][:2]
        to = dict(device_id={"seq": peer}, device_id_type=MESH)
        for i in range(count):
            yield pltpu.make_async_remote_copy(
                src_ref=lefts[c].at[strip_of(peer, orders[c], i)],
                dst_ref=lbuf.at[1, i],
                send_sem=xsend.at[c, 0],
                recv_sem=xrecv.at[c, 0],
                **to,
            )
        yield pltpu.make_async_remote_copy(
            src_ref=rights[c],
            dst_ref=rbuf.at[1],
            send_sem=xsend.at[c, 1],
            recv_sem=xrecv.at[c, 1],
            **to,
        )

    def settle(ref, sem):
        pltpu.make_async_copy(ref, ref, sem).wait()

    def halve(c, k):
        return pltpu.make_async_remote_copy(
            src_ref=pools[c][5 + 2 * k],
            dst_ref=pools[c][6 + 2 * k],
            send_sem=hsend.at[c, k],
            recv_sem=hrecv.at[c, k],
            device_id={"seq": flipped(me, orders[c][k])},
            device_id_type=MESH,
        )

    def across(c, j):
        to = lax.rem(w + j, n_w)
        return pltpu.make_async_remote_copy(
            src_ref=pools[c][3].at[to],
            dst_ref=pools[c][4].at[j - 1],
            send_sem=zsend.at[c, j - 1],
            recv_sem=zrecv.at[c, j - 1],
            device_id={"wshard": to},
            device_id_type=MESH,
        )

    def compute(c):
        lbuf, rbuf, part = pools[c][:3]
        settle(lbuf.at[0], load_sem.at[c, 0])
        settle(rbuf.at[0], load_sem.at[c, 1])
        settle(lbuf.at[1], xrecv.at[c, 0])
        settle(rbuf.at[1], xrecv.at[c, 1])
        height, rows = lbuf.shape[2:]
        width = rbuf.shape[2]
        step = column_step(width)
        half = count // 2
        groups = [(0, count)] if height % 16 == 0 else [(i, 1) for i in range(count)]

        @pl.loop(0, width // step)
        def _(t):
            cols = pl.ds(pl.multiple_of(t * step, step), step)
            for start, size in groups:
                total = None
                for h in range(2):
                    left = lbuf[h, start : start + size].reshape(size * height, rows)
                    term = dot_f32(left, rbuf[h, :, cols], ((1,), (0,)))
                    total = term if total is None else total + term
                total = total.reshape(size, height, step)
                for i in range(size):
                    at = start + i
                    if at < half:
                        pools[c][5][at, :, cols] = total[i].astype(jnp.bfloat16)
                    else:
                        part[at - half, :, cols] = total[i]

        halve(c, 0).start()

    def reduce(c, k):
        part = pools[c][2]
        settle(pools[c][6 + 2 * (k - 1)], hrecv.at[c, k - 1])
        got = pools[c][6 + 2 * (k - 1)]
        left = count >> k
        first = part.shape[0] - left
        send = left // 2
        if k < m:
            for i in range(left):
                value = part[first + i] + got[i].astype(jnp.float32)
                if i < send:
                    pools[c][5 + 2 * k][i] = value.astype(jnp.bfloat16)
                else:
                    part[first + i] = value
            halve(c, k).start()
            return
        value = part[first] + got[0].astype(jnp.float32)
        width = pools[c][3].shape[2]
        for i in range(n_w):
            pools[c][3][i] = value[:, i * width : (i + 1) * width].astype(jnp.bfloat16)
        for j in range(1, n_w):
            across(c, j).start()

    def finish(c):
        total = pools[c][3][w].astype(jnp.float32)
        for j in range(1, n_w):
            settle(pools[c][4].at[j - 1], zrecv.at[c, j - 1])
            total = total + pools[c][4][j - 1].astype(jnp.float32)
        outs[c][...] = total * scale

    greet(n_seq, n_w, me, w)
    for c in range(n):
        for copy in trades(c):
            copy.start()
        for copy in own_loads(c):
            copy.start()
    lag = 2
    for slot in range(n + lag * (m + 1)):
        for k in reversed(range(m + 2)):
            c = slot - lag * k
            if not 0 <= c < n:
                continue
            if k == 0:
                compute(c)
            elif k <= m:
                reduce(c, k)
            else:
                finish(c)
    for c in range(n):
        settle(pools[c][0].at[1], xsend.at[c, 0])
        settle(pools[c][1].at[1], xsend.at[c, 1])
        for k in range(m):
            halve(c, k).wait_send()
        for j in range(1, n_w):
            across(c, j).wait_send()


def sum_gradients(pairs, orders, n_seq, n_w, scale):
    n = len(pairs)
    m = n_seq.bit_length() - 2
    count = 1 << m
    lefts = [left.T.reshape(n_seq, left.shape[1] // n_seq, left.shape[0]) for left, _ in pairs]
    rights = [right for _, right in pairs]
    scratch = []
    outs = []
    for left, right in zip(lefts, rights):
        height, rows = left.shape[1:]
        width = right.shape[1]
        part = width // n_w
        scratch += [
            pltpu.VMEM((2, count, height, rows), jnp.bfloat16),
            pltpu.VMEM((2, rows, width), jnp.bfloat16),
            pltpu.VMEM((count // 2, height, width), jnp.float32),
            pltpu.VMEM((n_w, height, part), jnp.bfloat16),
            pltpu.VMEM((n_w - 1, height, part), jnp.bfloat16),
        ]
        for k in range(m):
            scratch += [pltpu.VMEM((count >> (k + 1), height, width), jnp.bfloat16)] * 2
        outs.append(jax.ShapeDtypeStruct((height, part), jnp.float32))
    dma = pltpu.SemaphoreType.DMA
    scratch += [dma((n, 2))] * 3 + [dma((n, m))] * 2 + [dma((n, n_w - 1))] * 2
    return pl.pallas_call(
        lambda *refs: sum_kernel(n_seq, n_w, orders, scale, *refs),
        out_shape=outs,
        in_specs=[pl.BlockSpec(memory_space=pl.ANY)] * (2 * n),
        out_specs=[pl.BlockSpec(memory_space=pltpu.VMEM)] * n,
        scratch_shapes=scratch,
        compiler_params=pltpu.CompilerParams(
            collective_id=1, has_side_effects=True, vmem_limit_bytes=67043328
        ),
    )(*lefts, *rights)


def sum_everywhere(values, axes):
    for axis in axes:
        count = lax.axis_size(axis)
        if count & (count - 1):
            values = lax.psum(values, axis)
            continue
        step = 1
        while step < count:
            pairs = [(i, i ^ step) for i in range(count)]
            values = values + lax.ppermute(values, axis, pairs)
            step *= 2
    return values


def per_device(
    tokens,
    attention_norm_gain,
    qkv_weight,
    output_weight,
    feedforward_norm_gain,
    input_weight,
    down_weight,
    cotangent,
):
    rows = tokens.shape[0]
    total_tokens = rows * lax.axis_size("seq") * lax.axis_size("wshard")
    length = total_tokens // SEQS
    block_index = lax.axis_index("seq") * lax.axis_size("wshard") + lax.axis_index("wshard")
    query_pos = block_index * rows + jnp.arange(rows, dtype=jnp.int32)
    begin = block_index * rows - WIN
    first = begin + WIN - (begin + WIN) % length
    bounds = jnp.stack([first - begin, first + length - begin]).astype(jnp.int32)
    cosine, sine = rope_tables(query_pos % length)
    scale_grad = 1.0 / math.sqrt(total_tokens)
    n_seq = lax.axis_size("seq")
    n_w = lax.axis_size("wshard")
    strip = D // n_seq
    col_qkv = qkv_weight.shape[2]
    col_out = output_weight.shape[2]
    col_in = input_weight.shape[2]
    row_down = down_weight.shape[1]

    order_a, order_b = [order + [0] for order in bit_orders(n_seq)]
    shares, orders = [], []
    for layer_number in range(LAYERS):
        for weight, order in ((qkv_weight, order_a), (input_weight, order_b)):
            shares.append(weight[layer_number].reshape(n_seq, strip, weight.shape[2]))
            orders.append(order)
        if layer_number == 0:
            shares.append(output_weight[0].reshape(n_seq, strip, col_out))
            orders.append(order_b)
            shares.append(down_weight.reshape(n_seq, LAYERS * row_down // n_seq, D))
            orders.append(order_a)
    for layer_number in range(1, LAYERS):
        shares.append(output_weight[layer_number].reshape(n_seq, strip, col_out))
        orders.append(order_b)
    wholes = gather_weights(shares, orders, n_seq, n_w)
    full_down_all = wholes[3].reshape(n_w, LAYERS, row_down, D)
    places = ((0, 1, 2), (4, 5, 6))
    gathered = []
    for layer_number in range(LAYERS):
        at_qkv, at_in, at_out = places[layer_number]
        gathered.append(
            (
                wholes[at_qkv].reshape(n_w, D, col_qkv),
                wholes[at_in].reshape(n_w, D, col_in),
                full_down_all[:, layer_number],
                wholes[at_out].reshape(n_w, D, col_out),
            )
        )

    def columns_product(left, weight):
        return jnp.concatenate(
            [jnp.dot(left, weight[i], preferred_element_type=jnp.float32) for i in range(n_w)],
            axis=1,
        )

    def rows_product(left, weight):
        return jnp.einsum(
            "twf,wdf->td",
            left.reshape(rows, n_w, weight.shape[2]),
            weight,
            preferred_element_type=jnp.float32,
        )

    hidden_state = tokens
    saved_activations = []
    for layer_number in range(LAYERS):
        full_qkv, full_in, full_down, full_out = gathered[layer_number]
        attention_standardized, attention_inverse_deviation = layer_normalize(hidden_state)
        attention_normalized = (attention_standardized * attention_norm_gain[layer_number]).astype(
            jnp.bfloat16
        )
        qkv = columns_product(attention_normalized, full_qkv)
        query_matrix, kv_rows = local_call(
            rope_kernel,
            [((rows, D), jnp.bfloat16), ((rows, 2 * D), jnp.bfloat16)],
            8 * rows * D,
            (qkv, cosine, sine),
        )
        padded = with_halo(kv_rows, ((("seq", "wshard"), 0),), WIN)
        context_rows, log_total = local_call(
            forward_kernel,
            [((rows, D), jnp.bfloat16), ((rows, HEADS), jnp.float32)],
            4 * rows * padded.shape[0] * D,
            (bounds, query_matrix, padded),
            True,
        )
        middle_state = hidden_state + columns_product(context_rows, full_out)
        feedforward_standardized, feedforward_inverse_deviation = layer_normalize(middle_state)
        feedforward_normalized = (
            feedforward_standardized * feedforward_norm_gain[layer_number]
        ).astype(jnp.bfloat16)
        inner_activation = columns_product(feedforward_normalized, full_in)
        gated_linear_output = (
            gelu_exact(inner_activation[:, :FF]) * inner_activation[:, FF:]
        ).astype(jnp.bfloat16)
        holding = None
        saved_activations.append(
            (
                holding,
                attention_standardized,
                attention_inverse_deviation,
                attention_normalized,
                query_matrix,
                padded,
                log_total,
                context_rows,
                feedforward_standardized,
                feedforward_inverse_deviation,
                feedforward_normalized,
                inner_activation,
                gated_linear_output,
            )
        )
        hidden_state = middle_state + jnp.dot(
            gated_linear_output, full_down.reshape(n_w * row_down, D), preferred_element_type=jnp.float32
        )
    grad = cotangent
    list_again, list_fgain, grad_pairs = ([], [], [])
    for layer_number in reversed(range(LAYERS)):
        (
            holding,
            attention_standardized,
            attention_inverse_deviation,
            attention_normalized,
            query_matrix,
            padded,
            log_total,
            context_rows,
            feedforward_standardized,
            feedforward_inverse_deviation,
            feedforward_normalized,
            inner_activation,
            gated_linear_output,
        ) = saved_activations[layer_number]
        full_qkv, full_in, full_down, full_out = gathered[layer_number]
        grad_rounded = grad.astype(jnp.bfloat16)
        grad_geglu = lax.dot_general(
            grad_rounded,
            full_down.reshape(n_w * row_down, D),
            (((1,), (1,)), ((), ())),
            preferred_element_type=jnp.float32,
        )
        gate = inner_activation[:, :FF]
        upper = inner_activation[:, FF:]
        grad_inner = jnp.concatenate(
            [grad_geglu * upper * gelu_slope(gate), grad_geglu * gelu_exact(gate)], axis=1
        ).astype(jnp.bfloat16)
        grad_pairs.append((feedforward_normalized, grad_inner))
        grad_pairs.append((grad_rounded, gated_linear_output))
        normalized_gradient = rows_product(grad_inner, full_in)
        partial_gradient, feedforward_gain_gradient = norm_backward_step(
            normalized_gradient,
            feedforward_standardized,
            feedforward_inverse_deviation,
            feedforward_norm_gain[layer_number],
        )
        list_fgain.append(feedforward_gain_gradient * scale_grad)
        grad_middle = grad + partial_gradient
        grad_middle_rounded = grad_middle.astype(jnp.bfloat16)
        grad_pairs.append((context_rows, grad_middle_rounded))
        grad_context = (
            rows_product(grad_middle_rounded, full_out).astype(jnp.bfloat16)
        )
        grad_queries, local_terms, rims = local_call(
            backward_kernel,
            [
                ((rows, D), jnp.float32),
                ((rows, 2 * D), jnp.float32),
                ((2 * WIN, 2 * D), jnp.bfloat16),
            ],
            10 * rows * padded.shape[0] * D,
            (bounds, query_matrix, padded, log_total, grad_context),
            True,
        )
        sites = ("seq", "wshard")
        count = lax.axis_size(sites)
        low = lax.ppermute(rims[WIN:], sites, [(i, i + 1) for i in range(count - 1)])
        high = lax.ppermute(rims[:WIN], sites, [(i + 1, i) for i in range(count - 1)])
        (grad_qkv,) = local_call(
            unrope_kernel,
            [((rows, 3 * D), jnp.bfloat16)],
            12 * rows * D,
            (grad_queries, local_terms, low, high, cosine, sine),
        )
        grad_pairs.append((attention_normalized, grad_qkv))
        attention_normalized_gradient = rows_product(grad_qkv, full_qkv)
        attention_partial_gradient, attention_gain_gradient = norm_backward_step(
            attention_normalized_gradient,
            attention_standardized,
            attention_inverse_deviation,
            attention_norm_gain[layer_number],
        )
        list_again.append(attention_gain_gradient * scale_grad)
        grad = grad_middle + attention_partial_gradient
    gain_sums = sum_everywhere(
        jnp.concatenate([jnp.stack(list_again[::-1]), jnp.stack(list_fgain[::-1])], axis=0),
        ("seq", "wshard"),
    )
    pair_orders = bit_orders(n_seq)
    summed = sum_gradients(
        grad_pairs, [pair_orders[(1, 0, 1, 0)[i % 4]] for i in range(len(grad_pairs))], n_seq, n_w, scale_grad
    )
    by_kind = [
        jnp.stack([summed[4 * (LAYERS - 1 - n) + kind] for n in range(LAYERS)]) for kind in (0, 1, 3, 2)
    ]
    return (
        hidden_state,
        grad,
        gain_sums[:LAYERS],
        by_kind[2],
        by_kind[3],
        gain_sums[LAYERS:],
        by_kind[0],
        jnp.swapaxes(by_kind[1], 1, 2),
    )


def solution(mesh):
    placed = (
        P(("seq", "wshard"), None),
        P(),
        P(None, None, "wshard"),
        P(None, None, "wshard"),
        P(),
        P(None, None, "wshard"),
        P(None, "wshard", None),
        P(("seq", "wshard"), None),
    )
    return jax.shard_map(
        per_device,
        mesh=mesh,
        in_specs=placed,
        out_specs=(
            P(("seq", "wshard"), None),
            P(("seq", "wshard"), None),
            P(),
            P(None, "seq", "wshard"),
            P(None, "seq", "wshard"),
            P(),
            P(None, "seq", "wshard"),
            P(None, "wshard", "seq"),
        ),
        check_vma=False,
    )
```
